32 devices in a mesh: dp: 16 (over z, x, core), tensor: 2 (over y).
Axes of the slice: x: 2, y: 2, z: 4, core: 2. Of those that a mesh axis runs over, the one named last changes fastest.
Arguments:
- hidden_in: bfloat16 [4096, 768], P(('dp', 'tensor')), may hold values from -6 to 6
- out_grad: bfloat16 [4096, 768], P(('dp', 'tensor')), may hold values from -6 to 6
- segment_ids: int32 [16, 256], P('dp'), may hold values from 0 to 3, never falling along the last dimension, each value on 1 to 128 neighbouring positions
- norm_weight: float32 [768], replicated, may hold values from 0.5 to 1.5
- w_z: bfloat16 [768, 1536], P('dp', 'tensor'), may hold values from -0.21875 to 0.21875
- w_x: bfloat16 [768, 1536], P('dp', 'tensor'), may hold values from -0.21875 to 0.21875
- w_bc: bfloat16 [768, 256], P('dp'), may hold values from -0.21875 to 0.21875
- w_dt: bfloat16 [768, 24], P('dp', 'tensor'), may hold values from -0.21875 to 0.21875
- conv_x_w: float32 [4, 1536], P(None, 'tensor'), may hold values from -0.5 to 0.5
- conv_x_b: float32 [1536], P('tensor'), may hold values from -0.5 to 0.5
- conv_bc_w: float32 [4, 256], replicated, may hold values from -0.5 to 0.5
- conv_bc_b: float32 [256], replicated, may hold values from -0.5 to 0.5
- dt_bias: float32 [24], P('tensor'), may hold values from -6 to -2.5
- a_log: float32 [24], P('tensor'), may hold values from 0 to 2.77
- d_skip: float32 [24], P('tensor'), may hold values from 0.5 to 1.5
- gnorm_weight: float32 [1536], P('tensor'), may hold values from 0.5 to 1.5
- w_out: bfloat16 [1536, 768], P('tensor', 'dp'), may hold values from -0.15625 to 0.15625
Outputs:
- block_out: bfloat16 [4096, 768], P(('dp', 'tensor'))
- grad_hidden: float32 [4096, 768], P(('dp', 'tensor'))
- grad_norm_weight: float32 [768], replicated
- grad_w_z: float32 [768, 1536], P('dp', 'tensor')
- grad_w_x: float32 [768, 1536], P('dp', 'tensor')
- grad_w_bc: float32 [768, 256], P('dp')
- grad_w_dt: float32 [768, 24], P('dp', 'tensor')
- grad_conv_x_w: float32 [4, 1536], P(None, 'tensor')
- grad_conv_x_b: float32 [1536], P('tensor')
- grad_conv_bc_w: float32 [4, 256], replicated
- grad_conv_bc_b: float32 [256], replicated
- grad_dt_bias: float32 [24], P('tensor')
- grad_a_log: float32 [24], P('tensor')
- grad_d_skip: float32 [24], P('tensor')
- grad_gnorm_weight: float32 [1536], P('tensor')
- grad_w_out: float32 [1536, 768], P('tensor', 'dp')
The draws below stay inside these ranges and needn't reach their ends.
Inputs may be any that keep to these rules, and one draw needn't show every extreme that they name: `segment_ids`: within a sequence the numbers start at 0, never fall and rise by one at each document start; each document has 1 to 128 tokens, one of them exactly 128.
All inputs are finite; a program needn't handle non-finite values.
Results may differ from the reference program's by a relative error of at most 0.017.
Values may be sent and summed in bfloat16 or wider, within the bound.
A program may use at most 128 MiB of HBM per device.

```python
import math
from functools import partial
import jax
import jax.numpy as jnp
import numpy as np
from jax import lax

D = 768
INNER = 1536
HEADS = 24
STATE = 128
CONV = 4
GROUP = 256
SEQ = 256
SEQS = 16
TOKENS = 4096


def block_scale(rng, dims, split, low, high):
    factor_of = 1.0
    for dim, blocks in split:
        draws = jax.random.uniform(jax.random.fold_in(jax.random.fold_in(rng, 6), dim), (blocks,), jnp.float32, low / len(split), high / len(split))
        factor_of = factor_of * jnp.repeat(jnp.exp(draws), dims[dim] // blocks).reshape((-1,) + (1,) * (len(dims) - 1 - dim))
    return factor_of


def profile(count, total, most, skew):
    loads = [(1 << 20) // math.isqrt(standing ** skew) + 1 for standing in range(2, count + 1)]
    rest, given = total - most - (count - 1), [1] * (count - 1)
    while rest > 0:
        free = [i for i in range(count - 1) if given[i] < most]
        whole, budget = sum([loads[i] for i in free]), rest
        for i in free:
            extra = min(most - given[i], max(1, budget * loads[i] // whole), rest)
            given[i] = given[i] + extra
            rest = rest - extra
    return np.array([most] + given)


def ragged(rng, number_of, total, limit, skew):
    if number_of == 2:
        one = jax.random.randint(rng, (), max(1, total - limit), min(limit, total - 1) + 1)
        return jnp.stack([one, total - one])
    tallies = jnp.asarray(profile(number_of, total, limit, skew), jnp.int32)
    twos = (number_of - 1) // 2
    donor, sink = tallies[1:1 + 2 * twos:2], tallies[2:2 + 2 * twos:2]
    room = jnp.minimum(donor - 1, limit - sink)
    passed = jax.random.randint(jax.random.fold_in(rng, 1), (twos,), 0, 1 << 20) % (room + 1)
    tallies = tallies.at[1:1 + 2 * twos:2].set(donor - passed).at[2:2 + 2 * twos:2].set(sink + passed)
    return tallies[jax.random.permutation(jax.random.fold_in(rng, 2), number_of)]


def gaussian(rng, shape, deviation, most, cuts=(), held_as=jnp.bfloat16):
    entries = deviation * jax.random.normal(rng, shape, jnp.float32)
    if cuts:
        entries = entries * block_scale(rng, shape, cuts, -0.22, 0.18)
    return jnp.clip(entries, -most, most).astype(held_as)


def setup_inputs(seed: int = 0) -> dict:
    splits = jax.random.split(jax.random.key(seed), 18)
    hidden_in = gaussian(splits[0], (TOKENS, D), 1.0, 6.0, ((0, 32),))
    out_grad = gaussian(splits[1], (TOKENS, D), 1.0, 6.0, ((0, 32),))
    segment_ids = jax.vmap(lambda own: jnp.searchsorted(jnp.cumsum(ragged(own, max(4, SEQ // 192), SEQ, SEQ // 2, 1)), jnp.arange(SEQ), side="right"))(jax.random.split(splits[2], SEQS)).reshape((SEQS, SEQ)).astype(jnp.int32)
    norm_weight = jnp.clip(1.0 + 0.1 * jax.random.normal(splits[3], (D,), jnp.float32), 0.5, 1.5)
    w_z = gaussian(splits[4], (D, INNER), D ** -0.5, 0.21875, ((0, 16), (1, 2)))
    w_x = gaussian(splits[5], (D, INNER), D ** -0.5, 0.21875, ((0, 16), (1, 2)))
    w_bc = gaussian(splits[6], (D, 2 * STATE), D ** -0.5, 0.21875, ((0, 16),))
    w_dt = gaussian(splits[7], (D, HEADS), D ** -0.5, 0.21875, ((0, 16), (1, 2)))
    conv_x_w = jnp.clip(jax.random.uniform(splits[8], (CONV, INNER), jnp.float32, -0.5, 0.5) * block_scale(splits[8], (CONV, INNER), ((1, 2),), -0.4, 0.0), -0.5, 0.5)
    conv_x_b = jnp.clip(jax.random.uniform(splits[9], (INNER,), jnp.float32, -0.5, 0.5) * block_scale(splits[9], (INNER,), ((0, 2),), -0.4, 0.0), -0.5, 0.5)
    conv_bc_w = jnp.clip(jax.random.uniform(splits[10], (CONV, 2 * STATE), jnp.float32, -0.5, 0.5), -0.5, 0.5)
    conv_bc_b = jnp.clip(jax.random.uniform(splits[11], (2 * STATE,), jnp.float32, -0.5, 0.5), -0.5, 0.5)
    dt_bias = jnp.clip(-6.0 + 3.5 * jax.random.uniform(splits[12], (HEADS,), jnp.float32) ** block_scale(splits[12], (HEADS,), ((0, 2),), -0.2, 0.2), -6.0, -2.5)
    a_log = jnp.clip(2.77 * jax.random.uniform(splits[13], (HEADS,), jnp.float32) ** block_scale(splits[13], (HEADS,), ((0, 2),), -0.2, 0.2), 0.0, 2.77)
    d_skip = jnp.clip(0.5 + 1.0 * jax.random.uniform(splits[14], (HEADS,), jnp.float32) ** block_scale(splits[14], (HEADS,), ((0, 2),), -0.2, 0.2), 0.5, 1.5)
    gnorm_weight = jnp.clip(1.0 + 0.1 * jax.random.normal(splits[15], (INNER,), jnp.float32), 0.5, 1.5)
    w_out = gaussian(splits[16], (INNER, D), INNER ** -0.5, 0.15625, ((0, 2), (1, 16)))
    return {"hidden_in": hidden_in, "out_grad": out_grad, "segment_ids": segment_ids, "norm_weight": norm_weight, "w_z": w_z, "w_x": w_x, "w_bc": w_bc, "w_dt": w_dt, "conv_x_w": conv_x_w, "conv_x_b": conv_x_b, "conv_bc_w": conv_bc_w, "conv_bc_b": conv_bc_b, "dt_bias": dt_bias, "a_log": a_log, "d_skip": d_skip, "gnorm_weight": gnorm_weight, "w_out": w_out}


epsilon = 1e-05

def shift_rows(values, offset):
    padding = jnp.zeros((offset, values.shape[1]), values.dtype)
    return jnp.concatenate([padding, values[:-offset]], axis=0)

def causal_conv(values, kernel, conv_bias, segments):
    kernel_taps = kernel.shape[0]
    summed = conv_bias[None, :] + kernel[kernel_taps - 1][None, :] * values
    for offset in range(1, kernel_taps):
        earlier = jnp.concatenate([jnp.full((offset,), -1, jnp.int32), segments[:-offset]])
        matches = (earlier == segments)[:, None]
        summed = summed + kernel[kernel_taps - 1 - offset][None, :] * jnp.where(matches, shift_rows(values, offset), 0.0)
    return jax.nn.silu(summed)

def group_scan(inputs, steps_dt, log_decay, in_state, out_state, segments, block_len):
    length, head_count, head_dim = inputs.shape
    blocks = length // block_len
    x_blocks = inputs.reshape(blocks, block_len, head_count, head_dim)
    dt_blocks = steps_dt.reshape(blocks, block_len, head_count)
    cum_decay = jnp.cumsum(log_decay.reshape(blocks, block_len, head_count), axis=1)
    b_blocks = in_state.reshape(blocks, block_len, -1)
    c_blocks = out_state.reshape(blocks, block_len, -1)
    seg_blocks = segments.reshape(blocks, block_len)
    positions = jnp.arange(block_len)
    causal = positions[:, None] >= positions[None, :]
    mask_intra = (causal[None] & (seg_blocks[:, :, None] == seg_blocks[:, None, :]))[:, None]
    scores = jnp.einsum('cqn,ckn->cqk', c_blocks, b_blocks, precision=lax.Precision.HIGHEST)
    cum_heads = cum_decay.transpose(0, 2, 1)
    differ = cum_heads[:, :, :, None] - cum_heads[:, :, None, :]
    decay_mat = jnp.where(mask_intra, jnp.exp(jnp.where(mask_intra, differ, 0.0)), 0.0)
    weights_mat = decay_mat * scores[:, None] * dt_blocks.transpose(0, 2, 1)[:, :, None, :]
    y_intra = jnp.einsum('chqk,ckhp->cqhp', weights_mat, x_blocks, precision=lax.Precision.HIGHEST)
    last_seg = seg_blocks[:, -1]
    to_end = cum_decay[:, -1:, :] - cum_decay
    end_match = (seg_blocks == last_seg[:, None])[:, :, None]
    end_weight = jnp.where(end_match, jnp.exp(jnp.where(end_match, to_end, 0.0)), 0.0) * dt_blocks
    local_states = jnp.einsum('ckh,ckhp,ckn->chpn', end_weight, x_blocks, b_blocks, precision=lax.Precision.HIGHEST)
    prev_last = jnp.concatenate([seg_blocks[:1, 0], last_seg[:-1]])
    carry_keep = jnp.where((last_seg == prev_last)[:, None], jnp.exp(cum_decay[:, -1, :]), 0.0)

    def advance(carried, packed):
        local_state, retain = packed
        return (retain[:, None, None] * carried + local_state, carried)
    zero_state = jnp.zeros(local_states.shape[1:], jnp.float32)
    _, entering = lax.scan(advance, zero_state, (local_states, carry_keep))
    start_match = (seg_blocks == prev_last[:, None])[:, :, None]
    start_weight = jnp.where(start_match, jnp.exp(cum_decay), 0.0)
    y_inter = jnp.einsum('cqn,chpn->cqhp', c_blocks, entering, precision=lax.Precision.HIGHEST) * start_weight[..., None]
    return (y_intra + y_inter).reshape(length, head_count, head_dim)

def mixer_core(z_proj, x_proj, bc_proj, dt_proj, conv_x_w, conv_x_b, conv_bc_w, conv_bc_b, dt_bias, a_log, d_skip, segments, block_len):
    head_count = dt_proj.shape[1]
    head_dim = x_proj.shape[1] // head_count
    state_dim = bc_proj.shape[1] // 2
    x_conv = causal_conv(x_proj, conv_x_w, conv_x_b, segments)
    bc_conv = causal_conv(bc_proj, conv_bc_w, conv_bc_b, segments)
    steps_dt = jax.nn.softplus(dt_proj + dt_bias[None, :])
    log_decay = -jnp.exp(a_log)[None, :] * steps_dt
    x_heads = x_conv.reshape(-1, head_count, head_dim)
    scanned = group_scan(x_heads, steps_dt, log_decay, bc_conv[:, :state_dim], bc_conv[:, state_dim:], segments, block_len)
    y_heads = scanned + d_skip[None, :, None] * x_heads
    return y_heads.reshape(x_proj.shape) * jax.nn.silu(z_proj)

def reference(hidden_in, out_grad, segment_ids, norm_weight, w_z, w_x, w_bc, w_dt, conv_x_w, conv_x_b, conv_bc_w, conv_bc_b, dt_bias, a_log, d_skip, gnorm_weight, w_out):
    seq_count, seq_len = segment_ids.shape
    model_width = hidden_in.shape[1]
    inner_all = w_z.shape[1]
    bc_width = w_bc.shape[1]
    w_cat = jnp.concatenate([w_z, w_x, w_bc, w_dt], axis=1)
    hidden_seq = hidden_in.reshape(seq_count, seq_len, model_width)
    cot_seq = out_grad.reshape(seq_count, seq_len, model_width)

    def one_sequence(totals, packed):
        hidden_rows, cot_rows, segments = packed
        hidden_f = hidden_rows.astype(jnp.float32)
        inv_rms = lax.rsqrt(lax.optimization_barrier(jnp.mean(hidden_f * hidden_f, axis=1, keepdims=True)) + epsilon)
        normed = (hidden_f * inv_rms * norm_weight[None, :]).astype(jnp.bfloat16)
        projected_all = jnp.dot(normed, w_cat, preferred_element_type=jnp.float32)
        z_proj = projected_all[:, :inner_all]
        x_proj = projected_all[:, inner_all:2 * inner_all]
        bc_proj = projected_all[:, 2 * inner_all:2 * inner_all + bc_width]
        dt_proj = projected_all[:, 2 * inner_all + bc_width:]
        core_fn = partial(mixer_core, segments=segments, block_len=GROUP)
        gated, core_vjp = jax.vjp(core_fn, z_proj, x_proj, bc_proj, dt_proj, conv_x_w, conv_x_b, conv_bc_w, conv_bc_b, dt_bias, a_log, d_skip)
        sq_sum = lax.optimization_barrier(jnp.sum(gated * gated, axis=1))
        inv_gate = lax.rsqrt(sq_sum / inner_all + epsilon)
        scaled_in = (gated * gnorm_weight[None, :]).astype(jnp.bfloat16)
        projected = jnp.dot(scaled_in, w_out, preferred_element_type=jnp.float32)
        block_rows = (hidden_f + inv_gate[:, None] * projected).astype(jnp.bfloat16)
        back_proj = jnp.dot(cot_rows, w_out.T, preferred_element_type=jnp.float32)
        inner_dot = lax.optimization_barrier(jnp.sum(back_proj * gated * gnorm_weight[None, :], axis=1))
        grad_q = inv_gate[:, None] * back_proj
        grad_gnorm = lax.optimization_barrier(jnp.sum(grad_q * gated, axis=0))
        cube_gate = inv_gate * inv_gate * inv_gate
        d_gated = grad_q * gnorm_weight[None, :] - (inner_dot * cube_gate / inner_all)[:, None] * gated
        scaled_out = (inv_gate[:, None] * scaled_in.astype(jnp.float32)).astype(jnp.bfloat16)
        grad_wout = jnp.dot(scaled_out.T, cot_rows, preferred_element_type=jnp.float32)
        core_grads = core_vjp(d_gated)
        d_proj = jnp.concatenate([part_grad.astype(jnp.bfloat16) for part_grad in core_grads[:4]], axis=1)
        grad_wcat = jnp.dot(normed.T, d_proj, preferred_element_type=jnp.float32)
        d_normed = jnp.dot(d_proj, w_cat.T, preferred_element_type=jnp.float32)
        grad_norm = lax.optimization_barrier(jnp.sum(d_normed * hidden_f * inv_rms, axis=0))
        d_scaled = d_normed * norm_weight[None, :]
        cube_rms = inv_rms * inv_rms * inv_rms
        grad_rows = cot_rows.astype(jnp.float32) + inv_rms * d_scaled - cube_rms * hidden_f * lax.optimization_barrier(jnp.mean(d_scaled * hidden_f, axis=1, keepdims=True))
        fresh = (grad_wcat, grad_wout, grad_norm, grad_gnorm) + tuple(core_grads[4:])
        new_totals = tuple((total_old + fresh_one for total_old, fresh_one in zip(totals, fresh)))
        return (new_totals, (block_rows, grad_rows))
    zero_totals = (jnp.zeros(w_cat.shape, jnp.float32), jnp.zeros(w_out.shape, jnp.float32), jnp.zeros(norm_weight.shape, jnp.float32), jnp.zeros(gnorm_weight.shape, jnp.float32), jnp.zeros(conv_x_w.shape, jnp.float32), jnp.zeros(conv_x_b.shape, jnp.float32), jnp.zeros(conv_bc_w.shape, jnp.float32), jnp.zeros(conv_bc_b.shape, jnp.float32), jnp.zeros(dt_bias.shape, jnp.float32), jnp.zeros(a_log.shape, jnp.float32), jnp.zeros(d_skip.shape, jnp.float32))
    totals, (block_all, grad_all) = lax.scan(one_sequence, zero_totals, (hidden_seq, cot_seq, segment_ids))
    grad_wcat = totals[0]
    block_out = block_all.reshape(seq_count * seq_len, model_width)
    grad_hidden = grad_all.reshape(seq_count * seq_len, model_width)
    return (block_out, grad_hidden, totals[2], grad_wcat[:, :inner_all], grad_wcat[:, inner_all:2 * inner_all], grad_wcat[:, 2 * inner_all:2 * inner_all + bc_width], grad_wcat[:, 2 * inner_all + bc_width:], totals[4], totals[5], totals[6], totals[7], totals[8], totals[9], totals[10], totals[3], totals[1])
```

```python
from functools import partial

import jax
import jax.numpy as jnp
from jax import lax
from jax.experimental import pallas as pl
from jax.experimental.pallas import tpu as pltpu
from jax.sharding import PartitionSpec as P

GROUP = 256


epsilon = 1e-05


def shift_rows(values, offset):
    padding = jnp.zeros((offset, values.shape[1]), values.dtype)
    return jnp.concatenate([padding, values[:-offset]], axis=0)


def causal_conv(values, kernel, conv_bias, segments):
    kernel_taps = kernel.shape[0]
    summed = conv_bias[None, :] + kernel[kernel_taps - 1][None, :] * values
    for offset in range(1, kernel_taps):
        earlier = jnp.concatenate([jnp.full((offset,), -1, jnp.int32), segments[:-offset]])
        matches = (earlier == segments)[:, None]
        summed = summed + kernel[kernel_taps - 1 - offset][None, :] * jnp.where(
            matches, shift_rows(values, offset), 0.0
        )
    return jax.nn.silu(summed)


def group_scan(inputs, steps_dt, log_decay, in_state, out_state, segments, block_len):
    length, head_count, head_dim = inputs.shape
    blocks = length // block_len
    x_blocks = inputs.reshape(blocks, block_len, head_count, head_dim)
    dt_blocks = steps_dt.reshape(blocks, block_len, head_count)
    cum_decay = jnp.cumsum(log_decay.reshape(blocks, block_len, head_count), axis=1)
    b_blocks = in_state.reshape(blocks, block_len, -1)
    c_blocks = out_state.reshape(blocks, block_len, -1)
    seg_blocks = segments.reshape(blocks, block_len)
    positions = jnp.arange(block_len)
    causal = positions[:, None] >= positions[None, :]
    mask_intra = (causal[None] & (seg_blocks[:, :, None] == seg_blocks[:, None, :]))[:, None]
    scores = jnp.einsum("cqn,ckn->cqk", c_blocks, b_blocks, precision=lax.Precision.HIGHEST)
    cum_heads = cum_decay.transpose(0, 2, 1)
    differ = cum_heads[:, :, :, None] - cum_heads[:, :, None, :]
    decay_mat = jnp.where(mask_intra, jnp.exp(jnp.where(mask_intra, differ, 0.0)), 0.0)
    weights_mat = decay_mat * scores[:, None] * dt_blocks.transpose(0, 2, 1)[:, :, None, :]
    y_intra = jnp.einsum("chqk,ckhp->cqhp", weights_mat, x_blocks, precision=lax.Precision.HIGHEST)
    if blocks == 1:
        return y_intra.reshape(length, head_count, head_dim)
    last_seg = seg_blocks[:, -1]
    to_end = cum_decay[:, -1:, :] - cum_decay
    end_match = (seg_blocks == last_seg[:, None])[:, :, None]
    end_weight = jnp.where(end_match, jnp.exp(jnp.where(end_match, to_end, 0.0)), 0.0) * dt_blocks
    local_states = jnp.einsum(
        "ckh,ckhp,ckn->chpn", end_weight, x_blocks, b_blocks, precision=lax.Precision.HIGHEST
    )
    prev_last = jnp.concatenate([seg_blocks[:1, 0], last_seg[:-1]])
    carry_keep = jnp.where((last_seg == prev_last)[:, None], jnp.exp(cum_decay[:, -1, :]), 0.0)

    def advance(carried, packed):
        local_state, retain = packed
        return (retain[:, None, None] * carried + local_state, carried)

    zero_state = jnp.zeros(local_states.shape[1:], jnp.float32)
    _, entering = lax.scan(advance, zero_state, (local_states, carry_keep))
    start_match = (seg_blocks == prev_last[:, None])[:, :, None]
    start_weight = jnp.where(start_match, jnp.exp(cum_decay), 0.0)
    y_inter = (
        jnp.einsum("cqn,chpn->cqhp", c_blocks, entering, precision=lax.Precision.HIGHEST)
        * start_weight[..., None]
    )
    return (y_intra + y_inter).reshape(length, head_count, head_dim)


def mixer_core(
    z_proj,
    x_proj,
    bc_proj,
    dt_proj,
    conv_x_w,
    conv_x_b,
    conv_bc_w,
    conv_bc_b,
    dt_bias,
    a_log,
    d_skip,
    segments,
    block_len,
):
    head_count = dt_proj.shape[1]
    head_dim = x_proj.shape[1] // head_count
    state_dim = bc_proj.shape[1] // 2
    x_conv = causal_conv(x_proj, conv_x_w, conv_x_b, segments)
    bc_conv = causal_conv(bc_proj, conv_bc_w, conv_bc_b, segments)
    steps_dt = jax.nn.softplus(dt_proj + dt_bias[None, :])
    log_decay = -jnp.exp(a_log)[None, :] * steps_dt
    x_heads = x_conv.reshape(-1, head_count, head_dim)
    scanned = group_scan(
        x_heads,
        steps_dt,
        log_decay,
        bc_conv[:, :state_dim],
        bc_conv[:, state_dim:],
        segments,
        block_len,
    )
    y_heads = scanned + d_skip[None, :, None] * x_heads
    return y_heads.reshape(x_proj.shape) * jax.nn.silu(z_proj)


F32 = jnp.float32
BF16 = jnp.bfloat16
MESH = pl.DeviceIdType.MESH


def ring_order(count):
    near = [1, count - 1] if count > 2 else [1]
    return [k for k in near if 0 < k < count] + list(range(2, count - 1))


def place(n):
    me = lax.axis_index("dp")
    return me, me // 4, (me // 2) % 2, me % 2


def greet(peers):
    barrier = pltpu.get_barrier_semaphore()
    for peer in peers:
        pl.semaphore_signal(barrier, inc=1, device_id=peer, device_id_type=MESH)
    pl.semaphore_wait(barrier, len(peers))


def remote(src, dst, send_sem, recv_sem, peer):
    return pltpu.make_async_remote_copy(
        src_ref=src,
        dst_ref=dst,
        send_sem=send_sem,
        recv_sem=recv_sem,
        device_id=peer,
        device_id_type=MESH,
    )


def peers_of(n, nt):
    me, z, x, c = place(n)
    t = lax.axis_index("tensor")
    zs = n // 4
    z_peer = {k: (((z + k) % zs) * 4 + x * 2 + c, t) for k in range(1, zs)}
    x_peer = (z * 4 + (1 - x) * 2 + c, t)
    c_peer = (z * 4 + x * 2 + (1 - c), t)
    t_peer = {k: (me, (t + k) % nt) for k in range(1, nt)}
    return z_peer, x_peer, c_peer, t_peer


def gather_body(n, nt, w_ref, h_ref, o_ref, w_all, h_all, o_all,
                zs_sem, zr_sem, xs_sem, xr_sem, cs_sem, cr_sem, ts_sem, tr_sem):
    me, z, x, c = place(n)
    t = lax.axis_index("tensor")
    zn = n // 4
    z_peer, x_peer, c_peer, t_peer = peers_of(n, nt)
    greet(list(z_peer.values()) + [x_peer, c_peer] + list(t_peer.values()))
    above, below = z_peer[1], z_peer[zn - 1]
    has_above, has_below = z < zn - 1, z > 0
    started = []

    def go(src, dst, send_sem, recv_sem, peer):
        copy = remote(src, dst, send_sem, recv_sem, peer)
        copy.start()
        started.append(copy)

    def z_go(src, dst, level, up):
        copy = remote(src, dst, zs_sem.at[level + (0 if up else zn)], zr_sem.at[level],
                      above if up else below)
        copy.start()

    @pl.when(has_above)
    def _():
        z_go(w_ref, w_all.at[me], z, True)

    @pl.when(has_below)
    def _():
        z_go(w_ref, w_all.at[me], z, False)

    remote(w_ref, w_all.at[me], xs_sem.at[z], xr_sem.at[z], x_peer).start()
    remote(w_ref, w_all.at[me], cs_sem.at[z], cr_sem.at[z], c_peer).start()
    for k in range(1, nt):
        go(h_ref, h_all.at[t], ts_sem.at[k], tr_sem.at[k], t_peer[k])
        go(o_ref, o_all.at[t], ts_sem.at[nt + k], tr_sem.at[nt + k], t_peer[k])
    w_all[pl.ds(me, 1)] = w_ref[...][None]
    h_all[pl.ds(t, 1)] = h_ref[...][None]
    o_all[pl.ds(t, 1)] = o_ref[...][None]

    def take(level, up):
        got = w_all.at[level * 4 + x * 2 + c]
        remote(got, got, zs_sem.at[level], zr_sem.at[level], above).wait_recv()

        @pl.when(has_above if up else has_below)
        def _():
            z_go(got, got, level, up)

        remote(got, got, xs_sem.at[level], xr_sem.at[level], x_peer).start()
        remote(got, got, cs_sem.at[level], cr_sem.at[level], c_peer).start()

    def cross(level):
        got = w_all.at[level * 4 + (1 - x) * 2 + c]
        remote(got, got, xs_sem.at[level], xr_sem.at[level], x_peer).wait_recv()
        remote(got, got, cs_sem.at[zn + level], cr_sem.at[zn + level], c_peer).start()

    def by_distance(visit):
        for s in range(1, zn):
            @pl.when(z - s >= 0)
            def _(s=s):
                visit(z - s, True)

            @pl.when(z + s < zn)
            def _(s=s):
                visit(z + s, False)

    by_distance(take)
    cross(z)
    by_distance(lambda level, up: cross(level))
    for half in range(2):
        side = x if half == 0 else 1 - x
        for level in range(zn):
            got = w_all.at[level * 4 + side * 2 + (1 - c)]
            j = half * zn + level
            remote(got, got, cs_sem.at[j], cr_sem.at[j], c_peer).wait_recv()
    for k in range(1, nt):
        got_h = h_all.at[(t + nt - k) % nt]
        got_o = o_all.at[(t + nt - k) % nt]
        remote(got_h, got_h, ts_sem.at[k], tr_sem.at[k], t_peer[k]).wait_recv()
        remote(got_o, got_o, ts_sem.at[nt + k], tr_sem.at[nt + k], t_peer[k]).wait_recv()
    for copy in started:
        copy.wait_send()
    for level in range(zn):
        sent = w_all.at[level * 4 + x * 2 + c]
        crossed = w_all.at[level * 4 + (1 - x) * 2 + c]
        remote(sent, sent, xs_sem.at[level], xr_sem.at[level], x_peer).wait_send()
        remote(sent, sent, cs_sem.at[level], cr_sem.at[level], c_peer).wait_send()
        remote(crossed, crossed, cs_sem.at[zn + level], cr_sem.at[zn + level], c_peer).wait_send()

        @pl.when((level <= z) & has_above)
        def _(level=level, sent=sent):
            remote(sent, sent, zs_sem.at[level], zr_sem.at[level], above).wait_send()

        @pl.when((level >= z) & has_below)
        def _(level=level, sent=sent):
            remote(sent, sent, zs_sem.at[zn + level], zr_sem.at[level], below).wait_send()


VM = pl.BlockSpec(memory_space=pltpu.VMEM)
DMA = pltpu.SemaphoreType.DMA


def gather_all(w_pack, hidden, cot):
    n, nt = lax.axis_size("dp"), lax.axis_size("tensor")
    zn = n // 4
    return pl.pallas_call(
        partial(gather_body, n, nt),
        out_shape=(
            jax.ShapeDtypeStruct((n,) + w_pack.shape, BF16),
            jax.ShapeDtypeStruct((nt,) + hidden.shape, BF16),
            jax.ShapeDtypeStruct((nt,) + cot.shape, BF16),
        ),
        in_specs=[VM] * 3,
        out_specs=(VM,) * 3,
        scratch_shapes=[
            DMA((2 * zn,)), DMA((zn,)), DMA((zn,)), DMA((zn,)),
            DMA((2 * zn,)), DMA((2 * zn,)), DMA((2 * nt,)), DMA((2 * nt,)),
        ],
        compiler_params=pltpu.CompilerParams(collective_id=0, has_side_effects=True),
        name="gather_all",
    )(w_pack, hidden, cot)


def pair_body(nt, p_ref, out_ref, got_ref, s_sem, r_sem):
    me = lax.axis_index("dp")
    t = lax.axis_index("tensor")
    peers = {k: (me, (t + k) % nt) for k in range(1, nt)}
    greet(list(peers.values()))
    copies = []
    for k in range(1, nt):
        copy = remote(p_ref, got_ref.at[t], s_sem.at[k], r_sem.at[k], peers[k])
        copy.start()
        copies.append(copy)
    got_ref[pl.ds(t, 1)] = p_ref[...][None]
    for k in range(1, nt):
        got = got_ref.at[(t + nt - k) % nt]
        remote(got, got, s_sem.at[k], r_sem.at[k], peers[k]).wait_recv()
    total = got_ref[0]
    for i in range(1, nt):
        total = total + got_ref[i]
    out_ref[...] = total
    for copy in copies:
        copy.wait_send()


def tensor_sum(values):
    nt = lax.axis_size("tensor")
    return pl.pallas_call(
        partial(pair_body, nt),
        out_shape=jax.ShapeDtypeStruct(values.shape, F32),
        in_specs=[VM],
        out_specs=VM,
        scratch_shapes=[pltpu.VMEM((nt,) + values.shape, F32), DMA((nt,)), DMA((nt,))],
        compiler_params=pltpu.CompilerParams(collective_id=1, has_side_effects=True),
        name="tensor_sum",
    )(values)


def reduce_body(n, nt, bc_width, g_ref, dn_ref, op_ref, sl_ref, ss_ref,
                g_out, dn_out, op_out, sl_out, ss_out,
                c_got, x_put, x_got, z_put, z_got, dn_got, op_got, bc_put, bc_got,
                sl_c, sl_xput, sl_x, sl_z, ss_t, ss_cput, ss_c, ss_xput, ss_x, ss_z,
                cs, cr, xs, xr, zs, zr, ts, tr):
    me, z, x, c = place(n)
    t = lax.axis_index("tensor")
    zn = n // 4
    z_peer, x_peer, c_peer, t_peer = peers_of(n, nt)
    order = ring_order(zn)
    order = order[2:] + order[:2]
    greet(list(z_peer.values()) + [x_peer, c_peer] + list(t_peer.values()))
    started = []

    def go(src, dst, send_sem, recv_sem, peer):
        copy = remote(src, dst, send_sem, recv_sem, peer)
        copy.start()
        started.append(copy)

    def arrived(dst, send_sem, recv_sem, peer):
        remote(dst, dst, send_sem, recv_sem, peer).wait_recv()

    def mine(k, side, core):
        return ((z + k) % zn) * 4 + side * 2 + core

    go(sl_ref, sl_c, cs.at[2 * zn], cr.at[2 * zn], c_peer)
    for k in range(1, nt):
        go(ss_ref, ss_t.at[t], ts.at[k], tr.at[k], t_peer[k])
    zorder = order + [0]
    for half in range(2):
        side = 1 - x if half == 0 else x
        for k in zorder:
            j = half * zn + k
            go(g_ref.at[mine(k, side, 1 - c)], c_got.at[j], cs.at[j], cr.at[j], c_peer)
    for k in range(1, nt):
        peer_t = (t + k) % nt
        go(dn_ref.at[peer_t], dn_got.at[t], ts.at[nt + k], tr.at[nt + k], t_peer[k])
        go(op_ref.at[peer_t], op_got.at[t], ts.at[2 * nt + k], tr.at[2 * nt + k], t_peer[k])
    ss_t[pl.ds(t, 1)] = ss_ref[...][None]

    def x_send(k):
        arrived(c_got.at[k], cs.at[k], cr.at[k], c_peer)
        part = g_ref[mine(k, 1 - x, c)].astype(F32) + c_got[k].astype(F32)
        x_put[k] = part.astype(BF16)
        go(x_put.at[k], x_got.at[k], xs.at[k], xr.at[k], x_peer)

    for k in zorder[:1]:
        x_send(k)
    arrived(sl_c, cs.at[2 * zn], cr.at[2 * zn], c_peer)
    sl_xput[...] = sl_ref[...] + sl_c[...]
    go(sl_xput, sl_x, xs.at[zn], xr.at[zn], x_peer)
    for k in range(1, nt):
        got = ss_t.at[(t + nt - k) % nt]
        arrived(got, ts.at[k], tr.at[k], t_peer[k])
    total = ss_t[0]
    for i in range(1, nt):
        total = total + ss_t[i]
    ss_cput[...] = total
    go(ss_cput, ss_c, cs.at[2 * zn + 1], cr.at[2 * zn + 1], c_peer)
    for k in zorder[1:2]:
        x_send(k)
    arrived(ss_c, cs.at[2 * zn + 1], cr.at[2 * zn + 1], c_peer)
    ss_xput[...] = ss_cput[...] + ss_c[...]
    go(ss_xput, ss_x, xs.at[zn + 1], xr.at[zn + 1], x_peer)
    for k in zorder[2:]:
        x_send(k)

    def z_send(k):
        j = zn + k
        arrived(c_got.at[j], cs.at[j], cr.at[j], c_peer)
        part = g_ref[mine(k, x, c)].astype(F32) + c_got[j].astype(F32)
        arrived(x_got.at[k], xs.at[k], xr.at[k], x_peer)
        part = part + x_got[k].astype(F32)
        if k == 0:
            g_out[...] = part
        else:
            z_put[k] = part.astype(BF16)
            go(z_put.at[k], z_got.at[k], zs.at[k], zr.at[k], z_peer[k])

    for k in zorder[:1]:
        z_send(k)
    arrived(sl_x, xs.at[zn], xr.at[zn], x_peer)
    sl_z[pl.ds(z, 1)] = (sl_xput[...] + sl_x[...])[None]
    for k in order:
        go(sl_z.at[z], sl_z.at[z], zs.at[zn + k], zr.at[zn + k], z_peer[k])
    arrived(ss_x, xs.at[zn + 1], xr.at[zn + 1], x_peer)
    ss_z[pl.ds(z, 1)] = (ss_xput[...] + ss_x[...])[None]
    for k in order:
        go(ss_z.at[z], ss_z.at[z], zs.at[2 * zn + k], zr.at[2 * zn + k], z_peer[k])
    for k in zorder[1:]:
        z_send(k)

    dn_total = dn_ref[t].astype(F32)
    op_total = op_ref[t].astype(F32)
    for k in range(1, nt):
        slot = (t + nt - k) % nt
        arrived(dn_got.at[slot], ts.at[nt + k], tr.at[nt + k], t_peer[k])
        arrived(op_got.at[slot], ts.at[2 * nt + k], tr.at[2 * nt + k], t_peer[k])
        dn_total = dn_total + dn_got[slot].astype(F32)
        op_total = op_total + op_got[slot].astype(F32)
    dn_out[...] = dn_total
    op_out[...] = op_total

    for k in order:
        slot = sl_z.at[(z + zn - k) % zn]
        arrived(slot, zs.at[zn + k], zr.at[zn + k], z_peer[k])
        slot = ss_z.at[(z + zn - k) % zn]
        arrived(slot, zs.at[2 * zn + k], zr.at[2 * zn + k], z_peer[k])
    sl_total, ss_total = sl_z[0], ss_z[0]
    for i in range(1, zn):
        sl_total = sl_total + sl_z[i]
        ss_total = ss_total + ss_z[i]
    sl_out[...] = sl_total
    ss_out[...] = ss_total

    for k in order:
        arrived(z_got.at[k], zs.at[k], zr.at[k], z_peer[k])
        g_out[...] += z_got[k].astype(F32)
    bc_put[...] = g_out[:, :bc_width].astype(BF16)
    for k in range(1, nt):
        go(bc_put, bc_got.at[t], ts.at[3 * nt + k], tr.at[3 * nt + k], t_peer[k])
    bc_got[pl.ds(t, 1)] = bc_put[...][None]
    for k in range(1, nt):
        got = bc_got.at[(t + nt - k) % nt]
        arrived(got, ts.at[3 * nt + k], tr.at[3 * nt + k], t_peer[k])
    total = bc_got[0].astype(F32)
    for i in range(1, nt):
        total = total + bc_got[i].astype(F32)
    g_out[:, :bc_width] = total
    for copy in started:
        copy.wait_send()


def reduce_all(grads, dn_part, out_part, small_loc, small_sh, bc_width):
    n, nt = lax.axis_size("dp"), lax.axis_size("tensor")
    zn = n // 4
    shard = grads.shape[1:]
    rows = dn_part.shape[1:]
    sl, ss = small_loc.shape, small_sh.shape
    V = pltpu.VMEM
    return pl.pallas_call(
        partial(reduce_body, n, nt, bc_width),
        out_shape=(
            jax.ShapeDtypeStruct(shard, F32),
            jax.ShapeDtypeStruct(rows, F32),
            jax.ShapeDtypeStruct(rows, F32),
            jax.ShapeDtypeStruct(sl, F32),
            jax.ShapeDtypeStruct(ss, F32),
        ),
        in_specs=[VM] * 5,
        out_specs=(VM,) * 5,
        scratch_shapes=[
            V((2 * zn,) + shard, BF16), V((zn,) + shard, BF16), V((zn,) + shard, BF16),
            V((zn,) + shard, BF16), V((zn,) + shard, BF16),
            V((nt,) + rows, BF16), V((nt,) + rows, BF16),
            V((shard[0], bc_width), BF16), V((nt, shard[0], bc_width), BF16),
            V(sl, F32), V(sl, F32), V(sl, F32), V((zn,) + sl, F32),
            V((nt,) + ss, F32), V(ss, F32), V(ss, F32), V(ss, F32), V(ss, F32), V((zn,) + ss, F32),
            DMA((2 * zn + 2,)), DMA((2 * zn + 2,)), DMA((zn + 2,)), DMA((zn + 2,)),
            DMA((3 * zn,)), DMA((3 * zn,)), DMA((4 * nt,)), DMA((4 * nt,)),
        ],
        compiler_params=pltpu.CompilerParams(collective_id=2, has_side_effects=True),
        name="reduce_all",
    )(grads, dn_part, out_part, small_loc, small_sh)


def pad_columns(values, width):
    return jnp.pad(values, ((0, 0), (0, width - values.shape[1])))


HIGH = lax.Precision.HIGHEST


def mm(a, b, dims=((1,), (0,)), precision=None):
    return lax.dot_general(a, b, (dims, ((), ())), precision=precision, preferred_element_type=F32)


def row_shift(values, offset):
    return pltpu.roll(values, offset % values.shape[0], axis=0)


def sigmoid(values):
    return 1.0 / (1.0 + jnp.exp(-values))


def conv_masks(seg_col, taps):
    length = seg_col.shape[0]
    seg_wide = jnp.broadcast_to(seg_col, (length, 128))
    position = lax.broadcasted_iota(jnp.int32, (length, 128), 0)
    masks = [None]
    for o in range(1, taps):
        same = (row_shift(seg_wide, o) == seg_wide) & (position >= o)
        masks.append(jnp.where(same, 1.0, 0.0)[:, :1])
    return masks


def conv_pre(values, kernel, bias, masks):
    taps = kernel.shape[0]
    total = bias + kernel[taps - 1 : taps] * values
    for o in range(1, taps):
        total = total + kernel[taps - 1 - o : taps - o] * (masks[o] * row_shift(values, o))
    return total


def conv_back(d_pre, values, kernel, masks):
    taps = kernel.shape[0]
    d_values = kernel[taps - 1 : taps] * d_pre
    rows = [jnp.sum(d_pre * values, axis=0, keepdims=True)]
    for o in range(1, taps):
        masked = masks[o] * d_pre
        rows.append(jnp.sum(masked * row_shift(values, o), axis=0, keepdims=True))
        d_values = d_values + kernel[taps - 1 - o : taps - o] * row_shift(masked, -o)
    return d_values, rows[::-1], jnp.sum(d_pre, axis=0, keepdims=True)


def head_map(lanes, channels, head_dim):
    head = lax.broadcasted_iota(jnp.int32, (lanes, channels), 0)
    channel = lax.broadcasted_iota(jnp.int32, (lanes, channels), 1)
    return jnp.where(channel // head_dim == head, 1.0, 0.0)


def prepare_body(bc_width, wbc, wdt, seg, nw, cxb, gnw, cbb, dtb, alog, dskip, pack, vec, segc):
    lanes = pack.shape[1] - bc_width
    heads = wdt.shape[0]
    head = lax.broadcasted_iota(jnp.int32, (heads, lanes), 0)
    lane = lax.broadcasted_iota(jnp.int32, (heads, lanes), 1)
    unit = jnp.where(head == lane, 1.0, 0.0).astype(BF16)
    pack[:, :bc_width] = wbc[...]
    pack[:, bc_width:] = mm(wdt[...], unit, ((0,), (0,))).astype(BF16)
    vec[...] = jnp.zeros(vec.shape, F32)
    for i, ref in enumerate((nw, cxb, gnw, cbb, dtb, alog, dskip)):
        vec[i : i + 1, : ref.shape[0]] = ref[...][None, :]
    segc[...] = jnp.broadcast_to(seg[...].astype(F32), (128, seg.shape[1])).T


def prepare(w_bc, w_dt, segments, vectors, lanes):
    rows, bc_width = w_bc.shape
    width = max(v.shape[0] for v in vectors)
    length = segments.shape[1]
    return pl.pallas_call(
        partial(prepare_body, bc_width),
        out_shape=(
            jax.ShapeDtypeStruct((rows, bc_width + lanes), BF16),
            jax.ShapeDtypeStruct((8, width), F32),
            jax.ShapeDtypeStruct((length, 128), F32),
        ),
        in_specs=[VM] * 10,
        out_specs=(VM,) * 3,
        name="prepare",
    )(w_bc, w_dt.T, segments, *vectors)


def mega_body(n, nt, heads, inner_all, bc_width, *refs):
    (wbd, wx, wz, wo, h_ref, o_ref, segc_ref, segr, cxw, cbw, vec,
     gbd_out, gx_out, gz_out, go_out, dn_out, op_out, sl_out, ss_out, gate_out,
     abd, ax, az, ao, h_all, o_all,
     bdraw, xraw, xpre_s, dsil_s, xconv_s, stepw_s, xstep_s, bcpre_s, bcconv_s, u_s, step_s, cum_s,
     scores_s, decay_s, y_s, back_s, zsil_s, zdsil_s, gated_s, scaled_s, sum_t, norm_s,
     dy_s, dx_s, dz_b, dx_b, dbd_b,
     g_bd, g_x, g_z, g_o, cg_bd, cg_x, cg_z, cg_o, xp_bd, xp_x, xp_z, xp_o, xg_bd, xg_x, xg_z, xg_o,
     zp_bd, zp_x, zp_z, zp_o, zg_bd, zg_x, zg_z, zg_o,
     op_s, dn_s, op_got, dn_got, bc_put, bc_got,
     sl_s, ss_s, sl_c, sl_xput, sl_x, sl_z, ss_t, ss_cput, ss_c, ss_xput, ss_x, ss_z,
     azs, azr, axs, axr, acs, acr, ys, yr, rcs, rcr, rxs, rxr, rzs, rzr, scs, scr, sxs, sxr, szs, szr) = refs
    me, z, x, c = place(n)
    t = lax.axis_index("tensor")
    zn = n // 4
    rows = wx.shape[0]
    width = h_ref.shape[1]
    inner = wx.shape[1]
    own_rows = h_ref.shape[0]
    lanes = wbd.shape[1] - bc_width
    head_dim = inner // heads
    state = bc_width // 2
    length = nt * own_rows
    taps = cxw.shape[0]
    z_peer, x_peer, c_peer, t_peer = peers_of(n, nt)
    above, below = z_peer[1], z_peer[zn - 1]
    has_above, has_below = z < zn - 1, z > 0
    greet(list(z_peer.values()) + [x_peer, c_peer] + list(t_peer.values()))
    started = []

    def go(src, dst, send_sem, recv_sem, peer):
        copy = remote(src, dst, send_sem, recv_sem, peer)
        copy.start()
        started.append(copy)

    def arrived(dst, send_sem, recv_sem, peer):
        remote(dst, dst, send_sem, recv_sem, peer).wait_recv()

    BD, X, Z, O = range(4)
    own = (wbd, wx, wz, wo)
    full = (abd, ax, az, ao)

    def slot(level, side, core):
        return pl.ds(pl.multiple_of((level * 4 + side * 2 + core) * rows, 16), rows)

    def z_go(src, dst, ti, level, up):
        remote(src, dst, azs.at[(2 * ti + (0 if up else 1)) * zn + level], azr.at[ti * zn + level],
               above if up else below).start()

    def x_go(src, dst, ti, level):
        remote(src, dst, axs.at[ti * zn + level], axr.at[ti * zn + level], x_peer).start()

    def c_go(src, dst, ti, half, level):
        j = (2 * ti + half) * zn + level
        remote(src, dst, acs.at[j], acr.at[j], c_peer).start()

    def send_own(ti):
        src, dst = own[ti], full[ti].at[slot(z, x, c)]

        @pl.when(has_above)
        def _():
            z_go(src, dst, ti, z, True)

        @pl.when(has_below)
        def _():
            z_go(src, dst, ti, z, False)

        x_go(src, dst, ti, z)
        c_go(src, dst, ti, 0, z)
        full[ti][slot(z, x, c), :] = src[...]

    def by_distance(s, visit):
        @pl.when(z - s >= 0)
        def _():
            visit(z - s, True)

        @pl.when(z + s < zn)
        def _():
            visit(z + s, False)

    def take(ti, s):
        def visit(level, up):
            got = full[ti].at[slot(level, x, c)]
            arrived(got, azs.at[2 * ti * zn + level], azr.at[ti * zn + level], above)

            @pl.when(has_above if up else has_below)
            def _():
                z_go(got, got, ti, level, up)

            x_go(got, got, ti, level)
            c_go(got, got, ti, 0, level)

        by_distance(s, visit)

    def cross(ti, s):
        def visit(level, up):
            got = full[ti].at[slot(level, 1 - x, c)]
            arrived(got, axs.at[ti * zn + level], axr.at[ti * zn + level], x_peer)
            c_go(got, got, ti, 1, level)

        if s == 0:
            visit(z, True)
        else:
            by_distance(s, visit)

    def complete(ti):
        for half in range(2):
            side = x if half == 0 else 1 - x
            for level in range(zn):
                j = (2 * ti + half) * zn + level
                arrived(full[ti].at[slot(level, side, 1 - c)], acs.at[j], acr.at[j], c_peer)

    def y_go(kind, src, dst, k):
        go(src, dst, ys.at[kind * nt + k], yr.at[kind * nt + k], t_peer[k])

    def y_got(kind, dst, k):
        arrived(dst, ys.at[kind * nt + k], yr.at[kind * nt + k], t_peer[k])

    def token_rows(i):
        return pl.ds(pl.multiple_of(i * own_rows, 16), own_rows)

    send_own(BD)
    send_own(X)
    for k in range(1, nt):
        y_go(0, h_ref, h_all.at[token_rows(t)], k)
        y_go(1, o_ref, o_all.at[token_rows(t)], k)
    send_own(Z)
    h_all[token_rows(t), :] = h_ref[...]
    o_all[token_rows(t), :] = o_ref[...]
    take(BD, 1)
    take(X, 1)
    send_own(O)
    segc = segc_ref[:, :1]
    nw, cxb, gnw = vec[0:1, :width], vec[1:2, :inner], vec[2:3, :inner]
    cbb, dtb = vec[3:4, :bc_width], vec[4:5, :lanes]
    alog, dskip = vec[5:6, :lanes], vec[6:7, :lanes]
    for k in range(1, nt):
        y_got(0, h_all.at[token_rows((t + nt - k) % nt)], k)
    hid = h_all[...].astype(F32)
    rms = lax.rsqrt(jnp.mean(hid * hid, axis=1, keepdims=True) + epsilon)
    norm_s[...] = (hid * rms * nw).astype(BF16)
    cross(BD, 0)
    cross(X, 0)
    for s in range(2, zn):
        take(BD, s)
        take(X, s)
        take(Z, s - 1)
    take(O, 1)
    for s in range(1, zn):
        cross(BD, s)
        cross(X, s)
        if s == 1:
            cross(Z, 0)
            cross(O, 0)
    if zn > 2:
        take(O, 2)
    take(Z, zn - 1)
    complete(BD)
    complete(X)

    masks = conv_masks(segc, taps)
    row = lax.broadcasted_iota(jnp.int32, (length, length), 0)
    col = lax.broadcasted_iota(jnp.int32, (length, length), 1)
    allowed = (row >= col) & (segc == segr[...].astype(F32))
    bdraw[...] = mm(norm_s[...], abd[...])
    xraw[...] = mm(norm_s[...], ax[...])
    bc_pre = conv_pre(bdraw[:, :bc_width], cbw[...], cbb, masks)
    bcpre_s[...] = bc_pre
    bc_conv = (bc_pre * sigmoid(bc_pre)).astype(BF16)
    bcconv_s[...] = bc_conv
    u = bdraw[:, bc_width:] + dtb
    step = jnp.maximum(u, 0.0) + jnp.log1p(jnp.exp(-jnp.abs(u)))
    u_s[...] = u
    step_s[...] = step
    rate = -jnp.exp(alog)
    cum_s[...] = mm(jnp.where(row >= col, 1.0, 0.0), rate * step, precision=HIGH)
    x_pre = conv_pre(xraw[...], cxw[...], cxb, masks)
    x_sig = sigmoid(x_pre)
    dsil_s[...] = x_sig * (1.0 + x_pre * (1.0 - x_sig))
    xconv_s[...] = x_pre * x_sig
    spread = head_map(lanes, inner, head_dim)
    stepw_s[...] = mm(step, spread, precision=HIGH)
    xstep_s[...] = (xconv_s[...] * stepw_s[...]).astype(BF16)
    skip = mm(jnp.broadcast_to(dskip, (8, lanes)), spread, precision=HIGH)[:1]
    scores_s[...] = jnp.where(allowed, mm(bc_conv[:, state:], bc_conv[:, :state], ((1,), (1,))), 0.0)
    for s in range(3, zn):
        take(O, s)
    cross(Z, 1)
    per = 128 // head_dim
    lane = lax.broadcasted_iota(jnp.int32, (length, 128), 1)
    groups = heads // per
    relays = [partial(cross, O, 1)]
    for s in range(2, zn):
        relays += [partial(cross, Z, s), partial(cross, O, s)]
    cum = cum_s[...]
    cum_t = cum.T
    for g in range(groups):
        cols = slice(g * 128, (g + 1) * 128)
        part = None
        for i in range(per):
            h = g * per + i
            decay = jnp.exp(jnp.where(allowed, cum[:, h : h + 1] - cum_t[h : h + 1, :], 0.0))
            decay_s[h] = decay
            one = mm((decay * scores_s[...]).astype(BF16), xstep_s[:, cols])
            part = one if part is None else jnp.where(lane < i * head_dim, part, one)
        y_s[:, cols] = part + skip[:, cols] * xconv_s[:, cols]
        if relays:
            relays.pop(0)()
    for relay in relays:
        relay()
    complete(Z)
    z_val = mm(norm_s[...], az[...])
    z_sig = sigmoid(z_val)
    zsil_s[...] = z_val * z_sig
    zdsil_s[...] = z_sig * (1.0 + z_val * (1.0 - z_sig))
    gated = y_s[...] * zsil_s[...]
    gated_s[...] = gated
    scaled_s[...] = (gated * gnw).astype(BF16)
    sq = jnp.sum(gated * gated, axis=1, keepdims=True)
    for k in range(1, nt):
        y_got(1, o_all.at[token_rows((t + nt - k) % nt)], k)
    complete(O)
    back_s[...] = mm(o_all[...], ao[...])
    dot = jnp.sum(back_s[...] * gated_s[...] * gnw, axis=1, keepdims=True)
    both = jnp.where(lane == 0, sq, jnp.where(lane == 1, dot, 0.0))
    sum_t[pl.ds(t, 1)] = both.T[:8][None]
    for k in range(1, nt):
        y_go(2, sum_t.at[t], sum_t.at[t], k)
    op_s[...] = mm(scaled_s[...], ao[...], ((1,), (1,))).astype(BF16)
    for k in range(1, nt):
        y_go(3, op_s.at[token_rows((t + k) % nt)], op_got.at[t], k)
    sl_s[...] = jnp.zeros(sl_s.shape, F32)
    ss_s[...] = jnp.zeros(ss_s.shape, F32)
    for k in range(1, nt):
        y_got(2, sum_t.at[(t + nt - k) % nt], k)
    total = sum_t[0]
    for i in range(1, nt):
        total = total + sum_t[i]
    sums = jnp.concatenate([total, jnp.zeros((120, length), F32)], axis=0).T
    inv = lax.rsqrt(sums[:, :1] / inner_all + epsilon)
    gate_out[...] = jnp.broadcast_to(inv, (length, 128))
    coef = sums[:, 1:2] * (inv * inv * inv) / inner_all

    grad = (g_bd, g_x, g_z, g_o)
    cgot = (cg_bd, cg_x, cg_z, cg_o)
    xput = (xp_bd, xp_x, xp_z, xp_o)
    xgot = (xg_bd, xg_x, xg_z, xg_o)
    zput = (zp_bd, zp_x, zp_z, zp_o)
    zgot = (zg_bd, zg_x, zg_z, zg_o)
    gout = (gbd_out, gx_out, gz_out, go_out)
    order = ring_order(zn)
    order = order[2:] + order[:2]
    zorder = order + [0]

    def mine(k, side, core):
        return slot((z + k) % zn, side, core)

    def c_send(ti):
        for half in range(2):
            side = 1 - x if half == 0 else x
            for k in zorder:
                j = half * zn + k
                go(grad[ti].at[mine(k, side, 1 - c)], cgot[ti].at[j], rcs.at[2 * zn * ti + j],
                   rcr.at[2 * zn * ti + j], c_peer)

    def x_send(ti, k):
        j = 2 * zn * ti + k
        arrived(cgot[ti].at[k], rcs.at[j], rcr.at[j], c_peer)
        part = grad[ti][mine(k, 1 - x, c), :].astype(F32) + cgot[ti][k].astype(F32)
        xput[ti][k] = part.astype(BF16)
        go(xput[ti].at[k], xgot[ti].at[k], rxs.at[zn * ti + k], rxr.at[zn * ti + k], x_peer)

    def z_send(ti, k):
        j = 2 * zn * ti + zn + k
        arrived(cgot[ti].at[zn + k], rcs.at[j], rcr.at[j], c_peer)
        part = grad[ti][mine(k, x, c), :].astype(F32) + cgot[ti][zn + k].astype(F32)
        arrived(xgot[ti].at[k], rxs.at[zn * ti + k], rxr.at[zn * ti + k], x_peer)
        part = part + xgot[ti][k].astype(F32)
        if k == 0:
            gout[ti][...] = part
        else:
            zput[ti][k] = part.astype(BF16)
            go(zput[ti].at[k], zgot[ti].at[k], rzs.at[zn * ti + k], rzr.at[zn * ti + k], z_peer[k])

    def z_done(ti):
        part = gout[ti][...]
        for k in order:
            arrived(zgot[ti].at[k], rzs.at[zn * ti + k], rzr.at[zn * ti + k], z_peer[k])
            part = part + zgot[ti][k].astype(F32)
        gout[ti][...] = part

    scaled_out = (inv * scaled_s[...].astype(F32)).astype(BF16)
    g_o[...] = mm(o_all[...], scaled_out, ((0,), (0,))).astype(BF16)
    c_send(O)
    grad_q = inv * back_s[...]
    sl_s[taps + 1 : taps + 2, :] = jnp.sum(grad_q * gated_s[...], axis=0, keepdims=True)
    d_gated = grad_q * gnw - coef * gated_s[...]
    dy_s[...] = d_gated * zsil_s[...]
    dz_b[...] = (d_gated * y_s[...] * zdsil_s[...]).astype(BF16)
    for k in zorder:
        x_send(O, k)
    g_z[...] = mm(norm_s[...], dz_b[...], ((0,), (0,))).astype(BF16)
    c_send(Z)
    relays = [lambda: [x_send(Z, k) for k in zorder]]
    relays += [partial(z_send, O, k) for k in zorder]

    d_scores = jnp.zeros((length, length), F32)
    row_sums = jnp.zeros((length, 128), F32)
    col_sums = []
    for g in range(groups):
        cols = slice(g * 128, (g + 1) * 128)
        dy = dy_s[:, cols]
        dy_b = dy.astype(BF16)
        part = None
        for i in range(per):
            h = g * per + i
            inside = (lane >= i * head_dim) & (lane < (i + 1) * head_dim)
            decay = decay_s[h]
            weight = decay * scores_s[...]
            d_weight = mm(jnp.where(inside, dy, 0.0).astype(BF16), xstep_s[:, cols], ((1,), (1,)))
            d_scores = d_scores + d_weight * decay
            flow = d_weight * weight
            row_sums = jnp.where(lane == h, jnp.sum(flow, axis=1, keepdims=True), row_sums)
            col_sums.append(jnp.sum(flow, axis=0, keepdims=True))
            one = mm(weight.astype(BF16), dy_b, ((0,), (0,)))
            part = one if part is None else jnp.where(lane < i * head_dim, part, one)
        dx_s[:, cols] = part
        if relays:
            relays.pop(0)()
    for relay in relays:
        relay()
    col_rows = jnp.concatenate(col_sums + [jnp.zeros((128 - heads, length), F32)], axis=0)
    d_cum = row_sums - col_rows.T
    row = lax.broadcasted_iota(jnp.int32, (length, length), 0)
    col = lax.broadcasted_iota(jnp.int32, (length, length), 1)
    allowed = (row >= col) & (segc == segr[...].astype(F32))
    d_log = mm(jnp.where(row <= col, 1.0, 0.0), d_cum, precision=HIGH)
    spread = head_map(lanes, inner, head_dim)
    d_step = mm((dx_s[...] * xconv_s[...]).astype(BF16), spread.astype(BF16), ((1,), (1,)))
    rate = -jnp.exp(alog)
    d_step = d_step + rate * d_log
    d_u = d_step * sigmoid(u_s[...])
    head_lane = lax.broadcasted_iota(jnp.int32, (length, lanes), 1)
    dbd_b[:, bc_width:] = jnp.where(head_lane < heads, d_u, 0.0).astype(BF16)
    masks = conv_masks(segc, taps)
    d_scores = jnp.where(allowed, d_scores, 0.0).astype(BF16)
    d_b = mm(d_scores, bcconv_s[:, state:], ((0,), (0,)))
    d_c = mm(d_scores, bcconv_s[:, :state])
    bc_pre = bcpre_s[...]
    bc_sig = sigmoid(bc_pre)
    d_bcpre = jnp.concatenate([d_b, d_c], axis=1) * (bc_sig * (1.0 + bc_pre * (1.0 - bc_sig)))
    d_bc, conv_rows, bias_row = conv_back(d_bcpre, bdraw[:, :bc_width], cbw[...], masks)
    dbd_b[:, :bc_width] = d_bc.astype(BF16)
    for k in range(taps):
        ss_s[k : k + 1, :bc_width] = conv_rows[k]
    ss_s[taps : taps + 1, :bc_width] = bias_row
    g_bd[...] = mm(norm_s[...], dbd_b[...], ((0,), (0,))).astype(BF16)
    c_send(BD)

    dy = dy_s[...]
    skip = mm(jnp.broadcast_to(dskip, (8, lanes)), spread, precision=HIGH)[:1]
    d_xpre = (dx_s[...] * stepw_s[...] + skip * dy) * dsil_s[...]
    d_x, conv_rows, bias_row = conv_back(d_xpre, xraw[...], cxw[...], masks)
    dx_b[...] = d_x.astype(BF16)
    for k in range(taps):
        sl_s[k : k + 1, :] = conv_rows[k]
    sl_s[taps : taps + 1, :] = bias_row
    for k in zorder:
        x_send(BD, k)
    g_x[...] = mm(norm_s[...], dx_b[...], ((0,), (0,))).astype(BF16)
    c_send(X)
    skip_row = jnp.sum(dy * xconv_s[...], axis=0, keepdims=True)
    d_skip = mm(jnp.broadcast_to(skip_row, (8, inner)), spread, ((1,), (1,)), precision=HIGH)[:1]
    sl_s[taps + 2 : taps + 3, :lanes] = jnp.sum(d_u, axis=0, keepdims=True)
    sl_s[taps + 3 : taps + 4, :lanes] = rate * jnp.sum(d_log * step_s[...], axis=0, keepdims=True)
    sl_s[taps + 4 : taps + 5, :lanes] = d_skip
    go(sl_s, sl_c, scs.at[0], scr.at[0], c_peer)
    for k in zorder[:2]:
        z_send(Z, k)
    for k in zorder:
        x_send(X, k)
    d_normed = mm(dz_b[...], az[...], ((1,), (1,))) + mm(dx_b[...], ax[...], ((1,), (1,)))
    d_normed = d_normed + mm(dbd_b[...], abd[...], ((1,), (1,)))
    dn_s[...] = d_normed.astype(BF16)
    for k in range(1, nt):
        y_go(4, dn_s.at[token_rows((t + k) % nt)], dn_got.at[t], k)
    hid = h_all[...].astype(F32)
    rms = lax.rsqrt(jnp.mean(hid * hid, axis=1, keepdims=True) + epsilon)
    ss_s[taps + 1 : taps + 2, :] = jnp.sum(d_normed * (hid * rms), axis=0, keepdims=True)
    ss_t[pl.ds(t, 1)] = ss_s[...][None]
    for k in range(1, nt):
        y_go(5, ss_s, ss_t.at[t], k)
    arrived(sl_c, scs.at[0], scr.at[0], c_peer)
    sl_xput[...] = sl_s[...] + sl_c[...]
    go(sl_xput, sl_x, sxs.at[0], sxr.at[0], x_peer)
    for k in zorder[2:]:
        z_send(Z, k)
    for k in range(1, nt):
        y_got(5, ss_t.at[(t + nt - k) % nt], k)
    total = ss_t[0]
    for i in range(1, nt):
        total = total + ss_t[i]
    ss_cput[...] = total
    go(ss_cput, ss_c, scs.at[1], scr.at[1], c_peer)
    for k in zorder[:2]:
        z_send(BD, k)
    arrived(ss_c, scs.at[1], scr.at[1], c_peer)
    ss_xput[...] = ss_cput[...] + ss_c[...]
    go(ss_xput, ss_x, sxs.at[1], sxr.at[1], x_peer)
    for k in zorder[2:]:
        z_send(BD, k)
    z_done(O)
    for k in range(1, nt):
        y_got(3, op_got.at[(t + nt - k) % nt], k)
    total = op_s[token_rows(t), :].astype(F32)
    for k in range(1, nt):
        total = total + op_got[(t + nt - k) % nt].astype(F32)
    op_out[...] = total
    for k in zorder[:1]:
        z_send(X, k)
    z_done(Z)
    for k in zorder[1:2]:
        z_send(X, k)
    z_done(BD)
    bc_put[...] = gbd_out[:, :bc_width].astype(BF16)
    for k in range(1, nt):
        y_go(6, bc_put, bc_got.at[t], k)
    for k in range(1, nt):
        y_got(4, dn_got.at[(t + nt - k) % nt], k)
    total = dn_s[token_rows(t), :].astype(F32)
    for k in range(1, nt):
        total = total + dn_got[(t + nt - k) % nt].astype(F32)
    dn_out[...] = total
    for k in zorder[2:]:
        z_send(X, k)
    arrived(sl_x, sxs.at[0], sxr.at[0], x_peer)
    sl_z[pl.ds(z, 1)] = (sl_xput[...] + sl_x[...])[None]
    arrived(ss_x, sxs.at[1], sxr.at[1], x_peer)
    ss_z[pl.ds(z, 1)] = (ss_xput[...] + ss_x[...])[None]
    for k in order:
        go(sl_z.at[z], sl_z.at[z], szs.at[k], szr.at[k], z_peer[k])
        go(ss_z.at[z], ss_z.at[z], szs.at[zn + k], szr.at[zn + k], z_peer[k])
    bc_got[pl.ds(t, 1)] = bc_put[...][None]
    for k in range(1, nt):
        y_got(6, bc_got.at[(t + nt - k) % nt], k)
    total = bc_got[0].astype(F32)
    for i in range(1, nt):
        total = total + bc_got[i].astype(F32)
    gbd_out[:, :bc_width] = total
    z_done(X)
    for k in order:
        arrived(sl_z.at[(z + zn - k) % zn], szs.at[k], szr.at[k], z_peer[k])
        arrived(ss_z.at[(z + zn - k) % zn], szs.at[zn + k], szr.at[zn + k], z_peer[k])
    sl_total, ss_total = sl_z[0], ss_z[0]
    for i in range(1, zn):
        sl_total = sl_total + sl_z[i]
        ss_total = ss_total + ss_z[i]
    sl_out[...] = sl_total
    ss_out[...] = ss_total

    for copy in started:
        copy.wait_send()
    for ti in range(4):
        for level in range(zn):
            sent = full[ti].at[slot(level, x, c)]
            crossed = full[ti].at[slot(level, 1 - x, c)]
            j = 2 * ti * zn + level
            remote(sent, sent, axs.at[ti * zn + level], axr.at[ti * zn + level], x_peer).wait_send()
            remote(sent, sent, acs.at[j], acr.at[j], c_peer).wait_send()
            remote(crossed, crossed, acs.at[j + zn], acr.at[j + zn], c_peer).wait_send()

            @pl.when((level <= z) & has_above)
            def _(j=j, ti=ti, level=level, sent=sent):
                remote(sent, sent, azs.at[j], azr.at[ti * zn + level], above).wait_send()

            @pl.when((level >= z) & has_below)
            def _(j=j, ti=ti, level=level, sent=sent):
                remote(sent, sent, azs.at[j + zn], azr.at[ti * zn + level], below).wait_send()


def mega(w_bd, w_x, w_z, w_o, hidden, cot, seg_col, segments, conv_x_w, conv_bc_w, vec, heads, inner_all,
         bc_width):
    n, nt = lax.axis_size("dp"), lax.axis_size("tensor")
    zn = n // 4
    rows, inner = w_x.shape
    own_rows, width = hidden.shape
    length = nt * own_rows
    taps = conv_x_w.shape[0]
    bd = w_bd.shape[1]
    lanes = bd - bc_width
    sl, ss = (taps + 5, inner), (taps + 2, width)
    V = pltpu.VMEM
    wide = (bd, inner, inner, inner)

    def sds(*shape):
        return jax.ShapeDtypeStruct(shape, F32)

    def each(*lead):
        return [V(lead + (cols,), BF16) for cols in wide]

    act = V((length, inner), F32)
    act_b = V((length, inner), BF16)
    return pl.pallas_call(
        partial(mega_body, n, nt, heads, inner_all, bc_width),
        out_shape=(
            sds(rows, bd), sds(rows, inner), sds(rows, inner), sds(rows, inner), sds(own_rows, width),
            sds(own_rows, width), sds(*sl), sds(*ss), sds(length, 128),
        ),
        in_specs=[VM] * 11,
        out_specs=(VM,) * 9,
        scratch_shapes=[
            *each(n * rows), V((length, width), BF16), V((length, width), BF16),
            V((length, bd), F32), act, act, act, act, act, act_b, V((length, bc_width), F32),
            V((length, bc_width), BF16), V((length, lanes), F32), V((length, lanes), F32),
            V((length, lanes), F32), V((length, length), F32), V((heads, length, length), F32), act, act,
            act, act, act, act_b, V((nt, 8, length), F32), V((length, width), BF16),
            act, act, act_b, act_b, V((length, bd), BF16),
            *each(n * rows), *each(2 * zn, rows), *each(zn, rows), *each(zn, rows), *each(zn, rows),
            *each(zn, rows),
            V((length, width), BF16), V((length, width), BF16), V((nt, own_rows, width), BF16),
            V((nt, own_rows, width), BF16), V((rows, bc_width), BF16), V((nt, rows, bc_width), BF16),
            V(sl, F32), V(ss, F32), V(sl, F32), V(sl, F32), V(sl, F32), V((zn,) + sl, F32),
            V((nt,) + ss, F32), V(ss, F32), V(ss, F32), V(ss, F32), V(ss, F32), V((zn,) + ss, F32),
            DMA((8 * zn,)), DMA((4 * zn,)), DMA((4 * zn,)), DMA((4 * zn,)), DMA((8 * zn,)), DMA((8 * zn,)),
            DMA((7 * nt,)), DMA((7 * nt,)), DMA((8 * zn,)), DMA((8 * zn,)), DMA((4 * zn,)), DMA((4 * zn,)),
            DMA((4 * zn,)), DMA((4 * zn,)), DMA((2,)), DMA((2,)), DMA((2,)), DMA((2,)),
            DMA((2 * zn,)), DMA((2 * zn,)),
        ],
        compiler_params=pltpu.CompilerParams(collective_id=3, has_side_effects=True),
        name="mega",
    )(w_bd, w_x, w_z, w_o, hidden, cot, seg_col, segments, conv_x_w, conv_bc_w, vec)


def finish_body(heads, bc_width, taps, gbd, gxs, gzs, gos, dn, op, sl, ss, hidden, cot, gate, vec,
                block, ghid, gnorm_in, gz, gx, gbc, gdt, gcxw, gcxb, gcbw, gcbb, gdtb, galog, gskip,
                ggn, gout):
    rows, width = hidden.shape
    start = pl.multiple_of(lax.axis_index("tensor") * rows, rows)
    hid = hidden[...].astype(F32)
    rms = lax.rsqrt(jnp.mean(hid * hid, axis=1, keepdims=True) + epsilon)
    block[...] = (hid + gate[pl.ds(start, rows), :][:, :1] * op[...]).astype(BF16)
    d_scaled = dn[...] * vec[0:1, :width]
    cube = rms * rms * rms
    ghid[...] = (
        cot[...].astype(F32)
        + rms * d_scaled
        - cube * hid * jnp.mean(d_scaled * hid, axis=1, keepdims=True)
    )
    own, lanes = gbd.shape[0], gbd.shape[1] - bc_width
    gbc[...] = gbd[:, :bc_width]
    fill = jnp.zeros((-own % 128, lanes), F32)
    gdt[...] = jnp.concatenate([gbd[:, bc_width:], fill], axis=0).T[:heads, :own]
    gz[...] = gzs[...]
    gx[...] = gxs[...]
    gout[...] = gos[...]
    gcxw[...] = sl[:taps]
    gcbw[...] = ss[:taps, :bc_width]
    gcxb[...] = sl[taps]
    ggn[...] = sl[taps + 1]
    gdtb[...] = sl[taps + 2, :heads]
    galog[...] = sl[taps + 3, :heads]
    gskip[...] = sl[taps + 4, :heads]
    gcbb[...] = ss[taps, :bc_width]
    gnorm_in[...] = ss[taps + 1]


def finish(summed, hidden, cot, vec, heads, bc_width, taps):
    rows, width = hidden.shape
    own, inner = summed[1].shape

    def sds(*shape):
        return jax.ShapeDtypeStruct(shape, F32)

    outs = (
        jax.ShapeDtypeStruct((rows, width), BF16), sds(rows, width), sds(width), sds(own, inner),
        sds(own, inner), sds(own, bc_width), sds(heads, own), sds(taps, inner), sds(inner),
        sds(taps, bc_width), sds(bc_width), sds(heads), sds(heads), sds(heads), sds(inner),
        sds(own, inner),
    )
    results = pl.pallas_call(
        partial(finish_body, heads, bc_width, taps),
        out_shape=outs,
        in_specs=[VM] * 12,
        out_specs=(VM,) * 16,
        name="finish",
    )(*summed[:8], hidden, cot, summed[8], vec)
    return (*results[:6], results[6].T, *results[7:-1], results[-1].T)


def per_device(
    hidden_in, out_grad, segment_ids, norm_weight, w_z, w_x, w_bc, w_dt, conv_x_w, conv_x_b,
    conv_bc_w, conv_bc_b, dt_bias, a_log, d_skip, gnorm_weight, w_out,
):
    n, nt = lax.axis_size("dp"), lax.axis_size("tensor")
    rows_own, width = hidden_in.shape
    inner_loc = w_z.shape[1]
    inner_all = inner_loc * nt
    bc_width = w_bc.shape[1]
    heads = w_dt.shape[1]
    dt_pad = -(-heads // 128) * 128
    z0 = bc_width + dt_pad
    tokens = nt * rows_own
    head_dim = inner_loc // heads
    fused = (
        tokens == GROUP and inner_loc % 128 == 0 and 128 % head_dim == 0 and bc_width % 256 == 0
        and w_out.shape[1] <= 128
    )
    if fused:
        w_bd, vec, seg_col = prepare(
            w_bc, w_dt, segment_ids,
            (norm_weight, conv_x_b, gnorm_weight, conv_bc_b, dt_bias, a_log, d_skip), dt_pad,
        )
        summed = mega(
            w_bd, w_x, w_z, w_out.T, hidden_in, out_grad, seg_col, segment_ids, conv_x_w, conv_bc_w,
            vec, heads, inner_all, bc_width,
        )
        return finish(summed, hidden_in, out_grad, vec, heads, bc_width, conv_x_w.shape[0])
    w_pack = jnp.concatenate([w_bc, pad_columns(w_dt, dt_pad), w_z, w_x, w_out.T], axis=1)
    w_all, hid_all, cot_all = gather_all(w_pack, hidden_in, out_grad)
    w_full = w_all.reshape(width, -1)
    w_cat = w_full[:, : z0 + 2 * inner_loc]
    w_out_t = w_full[:, z0 + 2 * inner_loc :]
    cot_all = cot_all.reshape(tokens, width)
    hid_all = hid_all.reshape(tokens, width)
    hid_all = hid_all.astype(F32)
    rms_all = lax.rsqrt(jnp.mean(hid_all * hid_all, axis=1, keepdims=True) + epsilon)
    unit_all = hid_all * rms_all
    normed_all = (unit_all * norm_weight[None, :]).astype(BF16)
    projected_all = jnp.dot(normed_all, w_cat, preferred_element_type=F32)
    bc_proj = projected_all[:, :bc_width]
    dt_proj = projected_all[:, bc_width : bc_width + heads]
    z_proj = projected_all[:, z0 : z0 + inner_loc]
    x_proj = projected_all[:, z0 + inner_loc : z0 + 2 * inner_loc]
    back_proj = jnp.dot(cot_all, w_out_t, preferred_element_type=F32)
    core_fn = partial(mixer_core, segments=segment_ids[0], block_len=GROUP)
    gated, core_vjp = jax.vjp(
        core_fn, z_proj, x_proj, bc_proj, dt_proj, conv_x_w, conv_x_b, conv_bc_w, conv_bc_b,
        dt_bias, a_log, d_skip,
    )
    back_gated = back_proj * gated
    sums = tensor_sum(
        jnp.stack(
            [jnp.sum(gated * gated, axis=1), jnp.sum(back_gated * gnorm_weight[None, :], axis=1)]
        )
    )
    inv_gate = lax.rsqrt(sums[0] / inner_all + epsilon)
    cube_gate = inv_gate * inv_gate * inv_gate
    grad_gnorm = jnp.sum(inv_gate[:, None] * back_gated, axis=0)
    scaled_in = (gated * gnorm_weight[None, :]).astype(BF16)
    out_part = lax.dot_general(
        scaled_in, w_out_t, (((1,), (1,)), ((), ())), preferred_element_type=F32
    ).astype(BF16)
    d_gated = (inv_gate[:, None] * back_proj) * gnorm_weight[None, :] - (
        sums[1] * cube_gate / inner_all
    )[:, None] * gated
    scaled_out = (inv_gate[:, None] * scaled_in.astype(F32)).astype(BF16)
    core_grads = core_vjp(d_gated)
    d_z, d_x, d_bc, d_dt = [part.astype(BF16) for part in core_grads[:4]]
    d_proj = jnp.concatenate([d_bc, pad_columns(d_dt, dt_pad), d_z, d_x], axis=1)
    grad_wcat = lax.dot_general(
        normed_all, d_proj, (((0,), (0,)), ((), ())), preferred_element_type=F32
    ).astype(BF16)
    grad_wout_t = lax.dot_general(
        cot_all, scaled_out, (((0,), (0,)), ((), ())), preferred_element_type=F32
    ).astype(BF16)
    dn_part = lax.dot_general(
        d_proj, w_cat, (((1,), (1,)), ((), ())), preferred_element_type=F32
    )
    norm_part = jnp.sum(dn_part * unit_all, axis=0)
    grads = jnp.concatenate([grad_wcat, grad_wout_t], axis=1).reshape(n, width // n, -1)
    small_loc = jnp.concatenate(
        [
            core_grads[4],
            core_grads[5][None, :],
            grad_gnorm[None, :],
            *[pad_columns(core_grads[i][None, :], inner_loc) for i in (8, 9, 10)],
        ],
        axis=0,
    )
    small_sh = jnp.concatenate(
        [
            pad_columns(core_grads[6], width),
            pad_columns(core_grads[7][None, :], width),
            norm_part[None, :],
        ],
        axis=0,
    )
    dn_part, gate_all = dn_part.astype(BF16), inv_gate[:, None]
    g_own, d_normed, out_sum, small_loc, small_sh = reduce_all(
        grads,
        dn_part.reshape(nt, rows_own, width),
        out_part.reshape(nt, rows_own, width),
        small_loc,
        small_sh,
        bc_width,
    )
    row_start = lax.axis_index("tensor") * rows_own
    hidden_f = hidden_in.astype(F32)
    inv_rms = lax.rsqrt(jnp.mean(hidden_f * hidden_f, axis=1, keepdims=True) + epsilon)
    gate_own = lax.dynamic_slice_in_dim(gate_all, row_start, rows_own, 0)
    block_out = (hidden_f + gate_own * out_sum).astype(BF16)
    d_scaled = d_normed * norm_weight[None, :]
    cube_rms = inv_rms * inv_rms * inv_rms
    grad_hidden = (
        out_grad.astype(F32)
        + inv_rms * d_scaled
        - cube_rms * hidden_f * jnp.mean(d_scaled * hidden_f, axis=1, keepdims=True)
    )
    taps = conv_x_w.shape[0]
    return (
        block_out,
        grad_hidden,
        small_sh[taps + 1],
        g_own[:, z0 : z0 + inner_loc],
        g_own[:, z0 + inner_loc : z0 + 2 * inner_loc],
        g_own[:, :bc_width],
        g_own[:, bc_width : bc_width + heads],
        small_loc[:taps],
        small_loc[taps],
        small_sh[:taps, :bc_width],
        small_sh[taps, :bc_width],
        small_loc[taps + 2, :heads],
        small_loc[taps + 3, :heads],
        small_loc[taps + 4, :heads],
        small_loc[taps + 1],
        g_own[:, z0 + 2 * inner_loc :].T,
    )


def solution(mesh):
    in_specs = (
        P(("dp", "tensor"), None),
        P(("dp", "tensor"), None),
        P("dp", None),
        P(),
        P("dp", "tensor"),
        P("dp", "tensor"),
        P("dp", None),
        P("dp", "tensor"),
        P(None, "tensor"),
        P("tensor"),
        P(),
        P(),
        P("tensor"),
        P("tensor"),
        P("tensor"),
        P("tensor"),
        P("tensor", "dp"),
    )
    out_specs = (
        P(("dp", "tensor"), None),
        P(("dp", "tensor"), None),
        P(),
        P("dp", "tensor"),
        P("dp", "tensor"),
        P("dp", None),
        P("dp", "tensor"),
        P(None, "tensor"),
        P("tensor"),
        P(),
        P(),
        P("tensor"),
        P("tensor"),
        P("tensor"),
        P("tensor"),
        P("tensor", "dp"),
    )
    return jax.shard_map(
        per_device, mesh=mesh, in_specs=in_specs, out_specs=out_specs, check_vma=False
    )
```
